32 devices in a mesh: ctx: 8 (over z, y), wa: 4 (over x, core).
Axes of the slice: x: 2, y: 2, z: 4, core: 2. Of those that a mesh axis runs over, the one named last changes fastest.
Arguments:
- layer_input: bfloat16 [16, 2048, 768], P('wa', 'ctx'), may hold values from -6 to 6
- cotangent: bfloat16 [16, 2048, 768], P('wa', 'ctx'), may hold values from -12 to 12
- attention_gain: float32 [768], replicated, may hold values from 0.5 to 1.5
- qkv_proj: bfloat16 [768, 2304], P(None, 'wa'), may hold values from -0.21875 to 0.21875
- out_proj: bfloat16 [768, 768], P('wa'), may hold values from -0.875 to 0.875
- feed_gain: float32 [768], replicated, may hold values from 0.5 to 1.5
- in_proj: bfloat16 [768, 2304], P(None, 'wa'), may hold values from -0.21875 to 0.21875
- down_proj: bfloat16 [1152, 768], P('wa'), may hold values from -0.25 to 0.25
Outputs:
- output: bfloat16 [16, 2048, 768], P('wa', 'ctx')
- input_grad: float32 [16, 2048, 768], P('wa', 'ctx')
- attention_gain_grad: float32 [768], replicated
- feed_gain_grad: float32 [768], replicated
- qkv_proj_grad: float32 [768, 2304], P(None, 'wa')
- out_proj_grad: float32 [768, 768], P('wa')
- in_proj_grad: float32 [768, 2304], P(None, 'wa')
- down_proj_grad: float32 [1152, 768], P('wa')
The draws below stay inside these ranges and needn't reach their ends.
All inputs are finite; a program needn't handle non-finite values.
Results may differ from the reference program's by a relative error of at most 0.018.
Values may be sent and summed in bfloat16 or wider, within the bound.
No kernel may reach another device: no remote copies, remote signals or barrier semaphores. Data moves between devices by JAX's collectives and lax.ppermute only.
A program may use at most 192 MiB of HBM per device.

```python
import math
import jax
import jax.numpy as jnp
from jax import lax

D = 768
HEADS = 12
HEAD = 64
FF = 1152
HALF = 64
SEQS = 16
SEQ_LEN = 2048


def draw_cotangent(key, part):
    first_key = jax.random.fold_in(jax.random.fold_in(key, 7), 0)
    position = jnp.arange(SEQ_LEN, dtype=jnp.float32) / SEQ_LEN
    rising = jnp.exp(jnp.log(3.0) * position)[None, :, None]
    base_draw = jnp.clip(jax.random.normal(first_key, (SEQS, SEQ_LEN, D), jnp.float32), -4.0, 4.0)
    return (base_draw * rising).astype(jnp.bfloat16)


def level_of(key, extent, shards, smallest, largest):
    level, own = 1.0, jax.random.fold_in(key, 6)
    for dim, shards_of in shards:
        heights = jnp.exp(jax.random.uniform(jax.random.fold_in(own, dim), (shards_of,), jnp.float32, smallest / len(shards), largest / len(shards)))
        level = level * jnp.repeat(heights, extent[dim] // shards_of).reshape([-1 if axis == dim else 1 for axis in range(len(extent))])
    return level


def bell_draw(key, shape, scale, most, cuts=(), kind=jnp.bfloat16):
    entries = scale * jax.random.normal(key, shape, jnp.float32)
    if cuts:
        entries = entries * level_of(key, shape, cuts, -0.22, 0.18)
    return jnp.clip(entries, -most, most).astype(kind)


def setup_inputs(seed: int = 0) -> dict:
    streams_of = jax.random.split(jax.random.key(seed), 9)
    layer_input = bell_draw(streams_of[0], (SEQS, SEQ_LEN, D), 1.0, 6.0, ((0, 4), (1, 8)))
    cotangent = draw_cotangent(jax.random.fold_in(streams_of[8], 71), 0)
    attention_gain = jnp.clip(1.0 + 0.1 * jax.random.normal(streams_of[2], (D,), jnp.float32), 0.5, 1.5)
    qkv_proj = bell_draw(streams_of[3], (D, 3 * D), D ** -0.5, 0.21875, ((1, 4),))
    out_proj = bell_draw(streams_of[4], (D, D), (D // 16) ** -0.5, 0.875, ((0, 4),))
    feed_gain = jnp.clip(1.0 + 0.1 * jax.random.normal(streams_of[5], (D,), jnp.float32), 0.5, 1.5)
    in_proj = bell_draw(streams_of[6], (D, 2 * FF), D ** -0.5, 0.21875, ((1, 4),))
    down_proj = bell_draw(streams_of[7], (FF, D), (FF // 2) ** -0.5, 0.25, ((0, 4),))
    return {"layer_input": layer_input, "cotangent": cotangent, "attention_gain": attention_gain, "qkv_proj": qkv_proj, "out_proj": out_proj, "feed_gain": feed_gain, "in_proj": in_proj, "down_proj": down_proj}


@jax.custom_vjp
def low(v):
    return lax.optimization_barrier(v.astype(jnp.bfloat16)).astype(jnp.float32)

@jax.custom_vjp
def low_back(v):
    return v

def low_keep(v):
    return (low(v), None)

def low_pass(kept, grad):
    return (grad,)

def back_keep(v):
    return (v, None)

def back_low(kept, grad):
    return (low(grad),)
low.defvjp(low_keep, low_pass)
low_back.defvjp(back_keep, back_low)

def layer_stats(values):
    center = values - lax.optimization_barrier(jnp.mean(values, -1, keepdims=True))
    spread = lax.optimization_barrier(jnp.mean(center * center, -1, keepdims=True))
    return center * lax.rsqrt(spread + 1e-05)

def rotary_tables(places):
    frequencies = jnp.power(10000.0, -jnp.arange(0, HEAD, 2, dtype=jnp.float32) / HEAD)
    angles = places.astype(jnp.float32)[:, None] * frequencies[None, :]
    cosine = jnp.concatenate([jnp.cos(angles), jnp.cos(angles)], -1)
    sine = jnp.concatenate([jnp.sin(angles), jnp.sin(angles)], -1)
    return (cosine[:, None, :], sine[:, None, :])

def rotate(values, cosine, sine):
    half_len = HEAD // 2
    turned = jnp.concatenate([-values[..., half_len:], values[..., :half_len]], -1)
    return values * cosine + turned * sine

def attend(queries, keys, values):
    seq_len = queries.shape[0]
    block_rows = math.gcd(seq_len, 512)
    key_span = block_rows + 2 * HALF
    padded_keys = jnp.pad(keys, ((HALF, HALF), (0, 0), (0, 0)))
    padded_values = jnp.pad(values, ((HALF, HALF), (0, 0), (0, 0)))
    highest = lax.Precision.HIGHEST

    def one_block(start):
        query_block = lax.dynamic_slice_in_dim(queries, start, block_rows, 0)
        key_block = lax.dynamic_slice_in_dim(padded_keys, start, key_span, 0)
        value_block = lax.dynamic_slice_in_dim(padded_values, start, key_span, 0)
        query_place = start + jnp.arange(block_rows, dtype=jnp.int32)
        key_place = start - HALF + jnp.arange(key_span, dtype=jnp.int32)
        allowed = (jnp.abs(key_place[None, :] - query_place[:, None]) <= HALF) & ((key_place >= 0) & (key_place < seq_len))[None, :]
        scores = low_back(jnp.einsum('qhd,khd->hqk', query_block, key_block, precision=highest) * HEAD ** (-0.5))
        masked = jnp.where(allowed[None], scores, -1e+30)
        softmaxed = low(jax.nn.softmax(masked, axis=-1))
        return jnp.einsum('hqk,khd->qhd', softmaxed, value_block, precision=highest)
    starts = jnp.arange(seq_len // block_rows, dtype=jnp.int32) * block_rows
    blocks = lax.map(jax.checkpoint(one_block), starts)
    return blocks.reshape(seq_len, HEADS * HEAD)

def layer(tokens, first_gain, qkv_weight, out_weight, second_gain, in_weight, down_weight):
    highest = lax.Precision.HIGHEST
    seq_len = tokens.shape[0]
    model_width = HEADS * HEAD
    normed1 = low(layer_stats(tokens) * first_gain)
    projected = low_back(jnp.dot(normed1, qkv_weight, precision=highest))
    head_shape = (seq_len, HEADS, HEAD)
    cosine, sine = rotary_tables(jnp.arange(seq_len, dtype=jnp.int32))
    queries = low(rotate(projected[:, :model_width].reshape(head_shape), cosine, sine))
    keys = low(rotate(projected[:, model_width:2 * model_width].reshape(head_shape), cosine, sine))
    values = low(projected[:, 2 * model_width:].reshape(head_shape))
    attended = low(low_back(attend(queries, keys, values)))
    hidden1 = tokens + low_back(jnp.dot(attended, out_weight, precision=highest))
    normed2 = low(layer_stats(hidden1) * second_gain)
    inner = low_back(jnp.dot(normed2, in_weight, precision=highest))
    mixed = low(jax.nn.gelu(inner[:, :FF], approximate=False) * inner[:, FF:])
    return hidden1 + low_back(jnp.dot(mixed, down_weight, precision=highest))

def reference(layer_input, cotangent, attention_gain, qkv_proj, out_proj, feed_gain, in_proj, down_proj):
    params = tuple((entry_array.astype(jnp.float32) for entry_array in (attention_gain, qkv_proj, out_proj, feed_gain, in_proj, down_proj)))

    def one_sequence(totals, pair):
        tokens, grad_out = pair
        result, pullback = jax.vjp(layer, tokens, *params)
        grads = pullback(grad_out)
        totals = tuple((running + grad_piece for running, grad_piece in zip(totals, grads[1:])))
        return (totals, (result.astype(jnp.bfloat16), grads[0]))
    zero_list = tuple((jnp.zeros_like(entry_array) for entry_array in params))
    totals, (outputs, input_grads) = lax.scan(one_sequence, zero_list, (layer_input.astype(jnp.float32), cotangent.astype(jnp.float32)))
    return (outputs, input_grads, totals[0], totals[3], totals[1], totals[2], totals[4], totals[5])
```

```python
import functools
import math

import jax
import jax.numpy as jnp
from jax import lax
from jax.experimental import pallas as pl
from jax.experimental.pallas import tpu as pltpu
from jax.sharding import PartitionSpec as P

HEAD = 64
HALF = 64
QB = 128
LANES = 128
BF = jnp.bfloat16
F32 = jnp.float32
VMEM_LIMIT = 60 * 1024 * 1024
ANY = pl.BlockSpec(memory_space=pl.ANY)


def nn(a, b):
    return lax.dot_general(a, b, (((1,), (0,)), ((), ())), preferred_element_type=F32)


def nt(a, b):
    return lax.dot_general(a, b, (((1,), (1,)), ((), ())), preferred_element_type=F32)


def tn(a, b):
    return lax.dot_general(a, b, (((0,), (0,)), ((), ())), preferred_element_type=F32)


def params(n=1):
    return pltpu.CompilerParams(
        dimension_semantics=("arbitrary",) * n, vmem_limit_bytes=VMEM_LIMIT
    )


def cost(flops, nbytes, trans=0):
    return pl.CostEstimate(
        flops=int(flops), bytes_accessed=int(nbytes), transcendentals=int(trans)
    )


def fetch(rank, parts, full, sems):
    rows = parts[0].shape[0]
    copies = [
        pltpu.make_async_copy(
            part,
            full.at[pl.ds(pl.multiple_of((rank ^ j) * rows, 16), rows)],
            sems.at[j],
        )
        for j, part in enumerate(parts)
    ]
    for c in copies:
        c.start()
    return copies


def stats_of(values):
    center = values - jnp.mean(values, -1, keepdims=True)
    spread = jnp.mean(center * center, -1, keepdims=True)
    inverse = lax.rsqrt(spread + 1e-05)
    return center * inverse, inverse


def turn(u, cosine, sin_a, sin_b, back=False):
    turned = pltpu.roll(u, LANES - 32, 1) * sin_a + pltpu.roll(u, 32, 1) * sin_b
    return u * cosine - turned if back else u * cosine + turned


def two_heads(pair, low_lanes):
    zero = jnp.zeros_like(pair)
    return jnp.concatenate(
        [jnp.where(low_lanes, pair, zero), jnp.where(low_lanes, zero, pair)], 0
    )


def one_pair(stacked, low_lanes):
    half = stacked.shape[0] // 2
    return jnp.where(low_lanes, stacked[:half], stacked[half:])


def attend_kernel(
    n_parts, info, x_ref, left_ref, right_ref, gain_ref, cos_ref, sa_ref, sb_ref, *rest
):
    parts = rest[:n_parts]
    q_ref, k_ref, v_ref, att_ref, p_ref, lse_ref, normed_ref, full, normed, sems = rest[n_parts:]
    block = x_ref.shape[1]
    width = x_ref.shape[2]
    span = block + 2 * HALF
    pairs = width // LANES

    @pl.when(pl.program_id(0) == 0)
    def _():
        for c in fetch(info[0], parts, full, sems):
            c.wait()

    x = jnp.concatenate([left_ref[0], x_ref[0], right_ref[0]], 0).astype(F32)
    normal, _ = stats_of(x)
    normed[...] = (normal * gain_ref[...]).astype(BF)
    normed_ref[0] = normed[HALF : HALF + block]
    low_span = lax.broadcasted_iota(jnp.int32, (QB, LANES), 1) < HEAD
    for group in range(3 * pairs // 2):
        wide = nt(normed[...], full[group * 256 : (group + 1) * 256])
        for h in range(2):
            piece = wide[:, h * LANES : (h + 1) * LANES]
            which, pair = divmod(group * 2 + h, pairs)
            cols = slice(pair * LANES, (pair + 1) * LANES)
            if which < 2:
                piece = turn(piece, cos_ref[...], sa_ref[...], sb_ref[...])
            if which == 0:
                q_ref[0, :, cols] = (piece.astype(BF).astype(F32) * HEAD**-0.5).astype(BF)
            elif which == 1:
                k_ref[0, :, cols] = piece.astype(BF)
            else:
                v_ref[0, :, cols] = piece.astype(BF)
    query = lax.broadcasted_iota(jnp.int32, (QB, QB + 2 * HALF), 0)
    key = lax.broadcasted_iota(jnp.int32, (QB, QB + 2 * HALF), 1)
    lane = lax.broadcasted_iota(jnp.int32, (QB, LANES), 1)
    for qb in range(block // QB):
        place = info[1] * block + qb * QB - HALF + key
        allowed = (key >= query) & (key <= query + 2 * HALF) & (place >= 0) & (place < info[2])
        bias = jnp.where(allowed, 0.0, -1e30).astype(F32)
        bias = jnp.concatenate([bias, bias], 0)
        totals = jnp.zeros((QB, LANES), F32)
        own = slice(HALF + qb * QB, HALF + (qb + 1) * QB)
        keys = slice(qb * QB, (qb + 1) * QB + 2 * HALF)
        for pair in range(pairs):
            cols = slice(pair * LANES, (pair + 1) * LANES)
            scores = nt(two_heads(q_ref[0, own, cols], low_span), k_ref[0, keys, cols]) + bias
            top = jnp.max(scores, -1, keepdims=True)
            exps = jnp.exp(scores - top)
            total = jnp.sum(exps, -1, keepdims=True)
            soft = (exps * (1.0 / total)).astype(BF)
            p_ref[0, pair, qb] = soft
            att = one_pair(nn(soft, v_ref[0, keys, cols]), low_span)
            att_ref[0, qb * QB : (qb + 1) * QB, cols] = att.astype(BF)
            lse = top + jnp.log(total)
            totals = jnp.where(lane == 2 * pair, lse[:QB], totals)
            totals = jnp.where(lane == 2 * pair + 1, lse[QB:], totals)
        lse_ref[0, qb * QB : (qb + 1) * QB] = totals


def attend(info, x, left, right, gain, tables, parts):
    seqs, block, width = x.shape
    span = block + 2 * HALF
    pairs = width // LANES
    n = len(parts)
    rows = parts[0].shape[0]

    def seq(shape):
        return pl.BlockSpec((1,) + shape, lambda s, _: (s,) + (0,) * len(shape))

    def whole(shape):
        return pl.BlockSpec(shape, lambda s, _: (0,) * len(shape))

    table = whole((span, LANES))
    out = lambda *shape, t=BF: jax.ShapeDtypeStruct((seqs,) + shape, t)
    score_shape = (pairs, block // QB, 2 * QB, QB + 2 * HALF)
    return pl.pallas_call(
        functools.partial(attend_kernel, n),
        grid_spec=pltpu.PrefetchScalarGridSpec(
            num_scalar_prefetch=1,
            grid=(seqs,),
            in_specs=[
                seq((block, width)),
                seq((HALF, width)),
                seq((HALF, width)),
                whole((1, width)),
                table,
                table,
                table,
            ]
            + [ANY] * n,
            out_specs=[
                seq((span, width)),
                seq((span, width)),
                seq((span, width)),
                seq((block, width)),
                seq(score_shape),
                seq((block, LANES)),
                seq((block, width)),
            ],
            scratch_shapes=[
                pltpu.VMEM((n * rows, width), BF),
                pltpu.VMEM((span, width), BF),
                pltpu.SemaphoreType.DMA((n,)),
            ],
        ),
        out_shape=[
            out(span, width),
            out(span, width),
            out(span, width),
            out(block, width),
            out(*score_shape),
            out(block, LANES, t=F32),
            out(block, width),
        ],
        compiler_params=params(),
        cost_estimate=cost(seqs * span * width * width * 8, 30e6, 4e6),
        name="attend",
    )(info, x, left, right, gain, *tables, *parts)


def feed_kernel(
    n, hidden, info, x_ref, att_ref, cot_ref, lse_ref, gain_ref, ind_ref, *rest
):
    out_parts, in_parts, down_parts = rest[:n], rest[n : 2 * n], rest[2 * n : 3 * n]
    (
        output_ref,
        normed_ref,
        mixed_ref,
        inner_ref,
        grad_ref,
        branch_ref,
        dom_ref,
        gain_grad_ref,
        out_w,
        in_w,
        down_w,
        sems,
    ) = rest[3 * n :]
    width = x_ref.shape[2]
    first_step = pl.program_id(0) == 0

    @pl.when(first_step)
    def _():
        copies = fetch(info[0], out_parts, out_w, sems.at[0])
        copies += fetch(info[0], in_parts, in_w, sems.at[1])
        copies += fetch(info[0], down_parts, down_w, sems.at[2])
        for c in copies:
            c.wait()
        gain_grad_ref[...] = jnp.zeros_like(gain_grad_ref)

    attended = att_ref[0]
    hidden1 = x_ref[0].astype(F32) + nn(attended, out_w[...])
    normal, inverse = stats_of(hidden1)
    normed = (normal * gain_ref[...]).astype(BF)
    normed_ref[0] = normed
    cot = cot_ref[0]
    result = hidden1
    normed_grad = jnp.zeros_like(hidden1)
    step = 384
    for c in range(hidden // step):
        one = slice(c * step, (c + 1) * step)
        two = slice(hidden + c * step, hidden + (c + 1) * step)
        first = nt(normed, in_w[one])
        second = nt(normed, in_w[two])
        phi = 0.5 * (1.0 + lax.erf(first * (1.0 / math.sqrt(2.0))))
        active = first * phi
        slope = phi + first * jnp.exp(-0.5 * first * first) * (1.0 / math.sqrt(2.0 * math.pi))
        mixed = (active * second).astype(BF)
        mixed_ref[0, :, one] = mixed
        result = result + nn(mixed, down_w[one])
        mixed_grad = nt(cot, down_w[one])
        grad_one = (mixed_grad * second * slope).astype(BF)
        grad_two = (mixed_grad * active).astype(BF)
        inner_ref[0, :, one] = grad_one
        inner_ref[0, :, two] = grad_two
        normed_grad = normed_grad + nn(grad_one, in_w[one]) + nn(grad_two, in_w[two])
    output_ref[0] = result.astype(BF)
    gain_grad_ref[...] += jnp.sum(normed_grad * normal, 0, keepdims=True)
    scaled = normed_grad * gain_ref[...]
    hidden1_grad = cot.astype(F32) + inverse * (
        scaled
        - jnp.mean(scaled, -1, keepdims=True)
        - normal * jnp.mean(scaled * normal, -1, keepdims=True)
    )
    grad_ref[0] = hidden1_grad
    branch = hidden1_grad.astype(BF)
    branch_ref[0] = branch
    att_grad = nt(branch, out_w[...]).astype(BF)
    dom_ref[0, :, :width] = att_grad
    product = att_grad.astype(F32) * attended.astype(F32)
    high = product.astype(BF)
    rest_of = (product - high.astype(F32)).astype(BF)
    delta = nn(high, ind_ref[...]) + nn(rest_of, ind_ref[...])
    both = delta + lse_ref[0]
    high = both.astype(BF)
    rest_of = both - high.astype(F32)
    dom_ref[0, :, width:] = (high.astype(F32) + pltpu.roll(rest_of, 32, 1)).astype(BF)


def feed(info, x, att, cot, lse, gain, ind, out_parts, in_parts, down_parts):
    seqs, block, width = x.shape
    n = len(out_parts)
    hidden = n * down_parts[0].shape[0]

    def seq(*shape):
        return pl.BlockSpec((1,) + shape, lambda s, _: (s,) + (0,) * len(shape))

    def whole(*shape):
        return pl.BlockSpec(shape, lambda s, _: (0,) * len(shape))

    out = lambda *shape, t=BF: jax.ShapeDtypeStruct((seqs,) + shape, t)
    return pl.pallas_call(
        functools.partial(feed_kernel, n, hidden),
        grid_spec=pltpu.PrefetchScalarGridSpec(
            num_scalar_prefetch=1,
            grid=(seqs,),
            in_specs=[
                seq(block, width),
                seq(block, width),
                seq(block, width),
                seq(block, LANES),
                whole(1, width),
                whole(width, LANES),
            ]
            + [ANY] * (3 * n),
            out_specs=[
                seq(block, width),
                seq(block, width),
                seq(block, hidden),
                seq(block, 2 * hidden),
                seq(block, width),
                seq(block, width),
                seq(block, width + LANES),
                whole(1, width),
            ],
            scratch_shapes=[
                pltpu.VMEM((width, width), BF),
                pltpu.VMEM((2 * hidden, width), BF),
                pltpu.VMEM((hidden, width), BF),
                pltpu.SemaphoreType.DMA((3, n)),
            ],
        ),
        out_shape=[
            out(block, width),
            out(block, width),
            out(block, hidden),
            out(block, 2 * hidden),
            out(block, width, t=F32),
            out(block, width),
            out(block, width + LANES),
            jax.ShapeDtypeStruct((1, width), F32),
        ],
        compiler_params=params(),
        cost_estimate=cost(seqs * block * width * (4 * width + 12 * hidden), 30e6, 3e6),
        name="feed",
    )(info, x, att, cot, lse, gain, ind, *out_parts, *in_parts, *down_parts)


def attend_back_kernel(
    q_ref,
    k_ref,
    v_ref,
    p_ref,
    dom_ref,
    left_ref,
    right_ref,
    cos_ref,
    sa_ref,
    sb_ref,
    grad_ref,
):
    block = dom_ref.shape[1]
    width = q_ref.shape[2]
    span = block + 2 * HALF
    pairs = width // LANES
    scale = HEAD**-0.5
    low = lax.broadcasted_iota(jnp.int32, (QB, LANES), 1) < HEAD
    row = lax.broadcasted_iota(jnp.int32, (QB, QB), 0)
    col = lax.broadcasted_iota(jnp.int32, (QB, QB), 1)
    seen = ((row < HALF) & (col <= row)) | ((row >= HALF) & (col >= row))
    seen = jnp.concatenate([seen, seen], 0)
    stats = jnp.concatenate([left_ref[0, :, width:], right_ref[0, :, width:]], 0).astype(F32)
    stats = stats + pltpu.roll(stats, LANES - 32, 1)
    far = slice(HALF + block, span)
    near_left = slice(HALF, 2 * HALF)
    near_right = slice(block, block + HALF)
    blocks = block // QB
    for pair in range(pairs):
        cols = slice(pair * LANES, (pair + 1) * LANES)
        key_parts, value_parts = [], []
        for qb in range(blocks):
            own = slice(HALF + qb * QB, HALF + (qb + 1) * QB)
            keys = slice(qb * QB, (qb + 1) * QB + 2 * HALF)
            rows = slice(qb * QB, (qb + 1) * QB)
            soft = p_ref[0, pair, qb]
            att_grad = two_heads(dom_ref[0, rows, cols], low)
            soft_grad = nt(att_grad, v_ref[0, keys, cols])
            soft_wide = soft.astype(F32)
            delta = jnp.sum(soft_wide * soft_grad, -1, keepdims=True)
            score_grad = (soft_wide * (soft_grad - delta)).astype(BF)
            query_grad = one_pair(nn(score_grad, k_ref[0, keys, cols]), low) * scale
            grad_ref[0, rows, cols] = turn(
                query_grad, cos_ref[rows], sa_ref[rows], sb_ref[rows], True
            ).astype(BF)
            key_parts.append(tn(score_grad, two_heads(q_ref[0, own, cols], low)))
            value_parts.append(tn(soft, att_grad))
        far_q = two_heads(jnp.concatenate([q_ref[0, :HALF, cols], q_ref[0, far, cols]], 0), low)
        far_grad = two_heads(
            jnp.concatenate([left_ref[0, :, cols], right_ref[0, :, cols]], 0), low
        )
        near_k = jnp.concatenate([k_ref[0, near_left, cols], k_ref[0, near_right, cols]], 0)
        near_v = jnp.concatenate([v_ref[0, near_left, cols], v_ref[0, near_right, cols]], 0)
        h = 2 * pair
        lse = jnp.concatenate([stats[:, h : h + 1], stats[:, h + 1 : h + 2]], 0)
        delta = jnp.concatenate([stats[:, 64 + h : 65 + h], stats[:, 65 + h : 66 + h]], 0)
        soft = jnp.where(seen, jnp.exp(jnp.where(seen, nt(far_q, near_k) - lse, 0.0)), 0.0)
        score_grad = (soft * (nt(far_grad, near_v) - delta)).astype(BF)
        far_key = tn(score_grad, far_q)
        far_value = tn(soft.astype(BF), far_grad)
        for base, pieces, extra in ((width, key_parts, far_key), (2 * width, value_parts, far_value)):
            total = jnp.zeros((span, LANES), F32)
            for qb in range(blocks):
                before, after = qb * QB, span - (qb + 1) * QB - 2 * HALF
                piece = pieces[qb]
                if before:
                    piece = jnp.concatenate([jnp.zeros((before, LANES), F32), piece], 0)
                if after:
                    piece = jnp.concatenate([piece, jnp.zeros((after, LANES), F32)], 0)
                total = total + piece
            own = total[HALF : HALF + block]
            own = jnp.concatenate(
                [
                    own[:HALF] + extra[:HALF],
                    own[HALF : block - HALF],
                    own[block - HALF :] + extra[HALF:],
                ],
                0,
            )
            if base == width:
                own = turn(own, cos_ref[...], sa_ref[...], sb_ref[...], True)
            grad_ref[0, :, base + pair * LANES : base + (pair + 1) * LANES] = own.astype(BF)


def attend_back(q, k, v, p, dom, left, right, tables):
    seqs, block, _ = dom.shape
    span, width = q.shape[1:]

    def seq(*shape):
        return pl.BlockSpec((1,) + shape, lambda s: (s,) + (0,) * len(shape))

    table = pl.BlockSpec((block, LANES), lambda s: (0, 0))
    return pl.pallas_call(
        attend_back_kernel,
        grid=(seqs,),
        in_specs=[
            seq(span, width),
            seq(span, width),
            seq(span, width),
            seq(*p.shape[1:]),
            seq(block, width + LANES),
            seq(HALF, width + LANES),
            seq(HALF, width + LANES),
            table,
            table,
            table,
        ],
        out_specs=seq(block, 3 * width),
        out_shape=jax.ShapeDtypeStruct((seqs, block, 3 * width), BF),
        compiler_params=params(),
        cost_estimate=cost(seqs * block * span * width * 12, 25e6, 1e6),
        name="attend_back",
    )(q, k, v, p, dom, left, right, *tables)


def weight_grad_kernel(n, info, lhs_ref, rhs_ref, *rest):
    parts, full, sems = rest[:n], rest[n], rest[n + 1]
    rows = parts[0].shape[0]
    step = lhs_ref.shape[1]
    i = pl.program_id(0)
    full[pl.ds(pl.multiple_of(i * step, step), step)] = tn(lhs_ref[...], rhs_ref[...]).astype(BF)

    @pl.when(i == pl.num_programs(0) - 1)
    def _():
        copies = [
            pltpu.make_async_copy(
                full.at[pl.ds(pl.multiple_of((info[0] ^ j) * rows, 16), rows)],
                part,
                sems.at[j],
            )
            for j, part in enumerate(parts)
        ]
        for c in copies:
            c.start()
        for c in copies:
            c.wait()


def weight_grad(info, lhs, rhs, n):
    tokens, m = lhs.shape
    width = rhs.shape[1]
    step = 384
    return pl.pallas_call(
        functools.partial(weight_grad_kernel, n),
        grid_spec=pltpu.PrefetchScalarGridSpec(
            num_scalar_prefetch=1,
            grid=(m // step,),
            in_specs=[
                pl.BlockSpec((tokens, step), lambda i, _: (0, i)),
                pl.BlockSpec((tokens, width), lambda i, _: (0, 0)),
            ],
            out_specs=[ANY] * n,
            scratch_shapes=[pltpu.VMEM((m, width), BF), pltpu.SemaphoreType.DMA((n,))],
        ),
        out_shape=[jax.ShapeDtypeStruct((m // n, width), BF)] * n,
        compiler_params=params(),
        cost_estimate=cost(2 * tokens * m * width, 2 * (tokens * (m + width) + m * width)),
        name="weight_grad",
    )(info, lhs, rhs)


def input_kernel(n, info, grad_ref, x_ref, gain_ref, hidden_ref, *rest):
    parts = rest[:n]
    out_ref, gain_grad_ref, full, sems = rest[n:]

    @pl.when(pl.program_id(0) == 0)
    def _():
        for c in fetch(info[0], parts, full, sems):
            c.wait()
        gain_grad_ref[...] = jnp.zeros_like(gain_grad_ref)

    normed_grad = nn(grad_ref[0], full[...])
    normal, inverse = stats_of(x_ref[0].astype(F32))
    gain_grad_ref[...] += jnp.sum(normed_grad * normal, 0, keepdims=True)
    scaled = normed_grad * gain_ref[...]
    out_ref[0] = hidden_ref[0] + inverse * (
        scaled
        - jnp.mean(scaled, -1, keepdims=True)
        - normal * jnp.mean(scaled * normal, -1, keepdims=True)
    )


def input_back(info, grad, x, gain, hidden_grad, parts):
    seqs, block, width = x.shape
    n = len(parts)

    def seq(*shape):
        return pl.BlockSpec((1,) + shape, lambda s, _: (s,) + (0,) * len(shape))

    def whole(*shape):
        return pl.BlockSpec(shape, lambda s, _: (0,) * len(shape))

    return pl.pallas_call(
        functools.partial(input_kernel, n),
        grid_spec=pltpu.PrefetchScalarGridSpec(
            num_scalar_prefetch=1,
            grid=(seqs,),
            in_specs=[
                seq(block, 3 * width),
                seq(block, width),
                whole(1, width),
                seq(block, width),
            ]
            + [ANY] * n,
            out_specs=[seq(block, width), whole(1, width)],
            scratch_shapes=[
                pltpu.VMEM((3 * width, width), BF),
                pltpu.SemaphoreType.DMA((n,)),
            ],
        ),
        out_shape=[
            jax.ShapeDtypeStruct((seqs, block, width), F32),
            jax.ShapeDtypeStruct((1, width), F32),
        ],
        compiler_params=params(),
        cost_estimate=cost(seqs * block * width * width * 6, 16e6),
        name="input_back",
    )(info, grad, x, gain, hidden_grad, *parts)


def swap(value, axis, bit):
    count = lax.axis_size(axis)
    return lax.ppermute(value, axis, [(i, i ^ bit) for i in range(count)])


def bits_of(axis):
    count = lax.axis_size(axis)
    return [1 << b for b in range(count.bit_length() - 1)]


def gather_parts(shard):
    parts = {0: shard}
    for bit in reversed(bits_of("wa")):
        for j in list(parts):
            parts[j | bit] = swap(parts[j], "wa", bit)
    return [parts[j] for j in sorted(parts)]


def plus(a, b):
    return (a.astype(F32) + b.astype(F32)).astype(BF)


def reduce_parts(parts):
    parts = dict(enumerate(parts))
    for bit in bits_of("wa"):
        for j in [j for j in parts if j & bit]:
            parts[j ^ bit] = plus(parts[j ^ bit], swap(parts.pop(j), "wa", bit))
    value = parts[0]
    rank = lax.axis_index("ctx")
    bits = bits_of("ctx")
    cuts = bits[: min(2, len(bits) - 1)]
    for bit in cuts:
        half = value.shape[0] // 2
        mine = (rank & bit) // bit
        sent = lax.dynamic_slice_in_dim(value, (1 - mine) * half, half, 0)
        kept = lax.dynamic_slice_in_dim(value, mine * half, half, 0)
        value = plus(kept, swap(sent, "ctx", bit))
    for bit in bits[len(cuts) :]:
        value = plus(value, swap(value, "ctx", bit))
    for bit in reversed(cuts):
        mine = (rank & bit) // bit
        other = swap(value, "ctx", bit)
        value = jnp.where(
            mine == 0, jnp.concatenate([value, other], 0), jnp.concatenate([other, value], 0)
        )
    return value.astype(F32)


def sum_all(value):
    for axis in ("wa", "ctx"):
        for bit in bits_of(axis):
            value = value + swap(value, axis, bit)
    return value


def neighbours(value):
    count = lax.axis_size("ctx")
    ends = count - 1
    left = lax.ppermute(value[:, -HALF:], "ctx", [(i, i + 1) for i in range(ends)])
    right = lax.ppermute(value[:, :HALF], "ctx", [(i + 1, i) for i in range(ends)])
    return left, right


def local(
    layer_input, cotangent, attention_gain, qkv_proj, out_proj, feed_gain, in_proj, down_proj
):
    seqs, block, width = layer_input.shape
    rows = seqs * block
    heads = width // HEAD
    n = lax.axis_size("wa")
    context_rank = lax.axis_index("ctx")
    seq_len = block * lax.axis_size("ctx")
    info = jnp.stack(
        [
            lax.axis_index("wa").astype(jnp.int32),
            context_rank.astype(jnp.int32),
            jnp.int32(seq_len),
        ]
    )
    left, right = neighbours(layer_input)
    qkv_parts = gather_parts(qkv_proj.T)
    out_parts = gather_parts(out_proj)
    in_parts = gather_parts(in_proj.T)
    down_parts = gather_parts(down_proj)

    frequencies = jnp.power(10000.0, -jnp.arange(0, HEAD, 2, dtype=F32) / HEAD)
    places = context_rank * block - HALF + jnp.arange(block + 2 * HALF, dtype=jnp.int32)
    angles = places.astype(F32)[:, None] * frequencies[None, :]
    cosine, sine = jnp.cos(angles), jnp.sin(angles)
    zero = jnp.zeros_like(sine)
    tables = (
        jnp.concatenate([cosine] * 4, -1),
        jnp.concatenate([-sine, zero] * 2, -1),
        jnp.concatenate([zero, sine] * 2, -1),
    )
    own_tables = tuple(t[HALF : HALF + block] for t in tables)
    lane = jnp.arange(LANES, dtype=jnp.int32)[None, :]
    head_of = jnp.arange(width, dtype=jnp.int32)[:, None] // HEAD
    ind = (lane == head_of + 64).astype(BF)

    q, k, v, attended, soft, lse, normed1 = attend(
        info, layer_input, left, right, attention_gain[None], tables, qkv_parts
    )
    output, normed2, mixed, inner_grad, hidden_grad, branch, dom, feed_gain_grad = feed(
        info,
        layer_input,
        attended,
        cotangent,
        lse,
        feed_gain[None],
        ind,
        out_parts,
        in_parts,
        down_parts,
    )
    left_grad, right_grad = neighbours(dom)
    flat = lambda a: a.reshape(rows, a.shape[-1])
    in_grad = reduce_parts(weight_grad(info, flat(inner_grad), flat(normed2), n))
    down_grad = reduce_parts(weight_grad(info, flat(mixed), flat(cotangent), n))
    out_grad = reduce_parts(weight_grad(info, flat(attended), flat(branch), n))
    projected_grad = attend_back(q, k, v, soft, dom, left_grad, right_grad, own_tables)
    qkv_grad = reduce_parts(weight_grad(info, flat(projected_grad), flat(normed1), n))
    input_grad, attention_gain_grad = input_back(
        info, projected_grad, layer_input, attention_gain[None], hidden_grad, qkv_parts
    )
    gains = sum_all(
        jnp.concatenate([attention_gain_grad, feed_gain_grad], 0).reshape(-1, LANES)
    ).reshape(2, width)
    return (
        output,
        input_grad,
        gains[0],
        gains[1],
        qkv_grad.T,
        out_grad,
        in_grad.T,
        down_grad,
    )


def solution(mesh):
    return jax.shard_map(
        local,
        mesh=mesh,
        in_specs=(
            P("wa", "ctx", None),
            P("wa", "ctx", None),
            P(),
            P(None, "wa"),
            P("wa", None),
            P(),
            P(None, "wa"),
            P("wa", None),
        ),
        out_specs=(
            P("wa", "ctx", None),
            P("wa", "ctx", None),
            P(),
            P(),
            P(None, "wa"),
            P("wa", None),
            P(None, "wa"),
            P("wa", None),
        ),
        check_vma=False,
    )
```

```python
import functools
import math

import jax
import jax.numpy as jnp
from jax import lax
from jax.experimental import pallas as pl
from jax.experimental.pallas import tpu as pltpu
from jax.sharding import PartitionSpec as P

HEAD = 64
HALF = 64
QB = 128
LANES = 128
BF = jnp.bfloat16
F32 = jnp.float32
VMEM_LIMIT = 60 * 1024 * 1024
ANY = pl.BlockSpec(memory_space=pl.ANY)


def nn(a, b):
    return lax.dot_general(a, b, (((1,), (0,)), ((), ())), preferred_element_type=F32)


def nt(a, b):
    return lax.dot_general(a, b, (((1,), (1,)), ((), ())), preferred_element_type=F32)


def tn(a, b):
    return lax.dot_general(a, b, (((0,), (0,)), ((), ())), preferred_element_type=F32)


def params(n=1):
    return pltpu.CompilerParams(
        dimension_semantics=("arbitrary",) * n, vmem_limit_bytes=VMEM_LIMIT
    )


def cost(flops, nbytes, trans=0):
    return pl.CostEstimate(
        flops=int(flops), bytes_accessed=int(nbytes), transcendentals=int(trans)
    )


def start_all(copies):
    for c in copies:
        c.start()
    for c in copies:
        c.wait()


def load(rank, parts, full, sems, sizes):
    copies, taken, base = [], 0, 0
    for rows in sizes:
        for j, part in enumerate(parts):
            row = pl.multiple_of(base + (rank ^ j) * rows, 16)
            copies.append(
                pltpu.make_async_copy(
                    part.at[pl.ds(taken, rows)], full.at[pl.ds(row, rows)], sems.at[len(copies)]
                )
            )
        taken += rows
        base += rows * len(parts)
    start_all(copies)


def stats_of(values):
    center = values - jnp.mean(values, -1, keepdims=True)
    spread = jnp.mean(center * center, -1, keepdims=True)
    inverse = lax.rsqrt(spread + 1e-05)
    return center * inverse, inverse


def turn(u, cosine, sin_a, sin_b, back=False):
    turned = pltpu.roll(u, LANES - 32, 1) * sin_a + pltpu.roll(u, 32, 1) * sin_b
    return u * cosine - turned if back else u * cosine + turned


def two_heads(pair, low_lanes):
    zero = jnp.zeros_like(pair)
    return jnp.concatenate(
        [jnp.where(low_lanes, pair, zero), jnp.where(low_lanes, zero, pair)], 0
    )


def one_pair(stacked, low_lanes):
    half = stacked.shape[0] // 2
    return jnp.where(low_lanes, stacked[:half], stacked[half:])


def attend_kernel(
    info, x_ref, left_ref, right_ref, gain_ref, cos_ref, sa_ref, sb_ref, *rest
):
    parts = rest[:4]
    q_ref, k_ref, v_ref, att_ref, p_ref, lse_ref, normed_ref, full, normed, sems = rest[4:]
    block = x_ref.shape[1]
    width = x_ref.shape[2]
    span = block + 2 * HALF
    pairs = width // LANES

    @pl.when(pl.program_id(0) == 0)
    def _():
        load(info[0], parts, full, sems, (parts[0].shape[0],))

    x = jnp.concatenate([left_ref[0], x_ref[0], right_ref[0]], 0).astype(F32)
    normal, _ = stats_of(x)
    normed[...] = (normal * gain_ref[...]).astype(BF)
    normed_ref[0] = normed[HALF : HALF + block]
    low_span = lax.broadcasted_iota(jnp.int32, (QB, LANES), 1) < HEAD
    for group in range(3 * pairs // 2):
        wide = nt(normed[...], full[group * 256 : (group + 1) * 256])
        for h in range(2):
            piece = wide[:, h * LANES : (h + 1) * LANES]
            which, pair = divmod(group * 2 + h, pairs)
            cols = slice(pair * LANES, (pair + 1) * LANES)
            if which < 2:
                piece = turn(piece, cos_ref[...], sa_ref[...], sb_ref[...])
            if which == 0:
                q_ref[0, :, cols] = (piece.astype(BF).astype(F32) * HEAD**-0.5).astype(BF)
            elif which == 1:
                k_ref[0, :, cols] = piece.astype(BF)
            else:
                v_ref[0, :, cols] = piece.astype(BF)
    query = lax.broadcasted_iota(jnp.int32, (QB, QB + 2 * HALF), 0)
    key = lax.broadcasted_iota(jnp.int32, (QB, QB + 2 * HALF), 1)
    lane = lax.broadcasted_iota(jnp.int32, (QB, LANES), 1)
    for qb in range(block // QB):
        place = info[1] * block + qb * QB - HALF + key
        allowed = (key >= query) & (key <= query + 2 * HALF) & (place >= 0) & (place < info[2])
        bias = jnp.where(allowed, 0.0, -1e30).astype(F32)
        bias = jnp.concatenate([bias, bias], 0)
        totals = jnp.zeros((QB, LANES), F32)
        own = slice(HALF + qb * QB, HALF + (qb + 1) * QB)
        keys = slice(qb * QB, (qb + 1) * QB + 2 * HALF)
        for pair in range(pairs):
            cols = slice(pair * LANES, (pair + 1) * LANES)
            scores = nt(two_heads(q_ref[0, own, cols], low_span), k_ref[0, keys, cols]) + bias
            top = jnp.max(scores, -1, keepdims=True)
            exps = jnp.exp(scores - top)
            total = jnp.sum(exps, -1, keepdims=True)
            soft = (exps * (1.0 / total)).astype(BF)
            p_ref[0, pair, qb] = soft
            att = one_pair(nn(soft, v_ref[0, keys, cols]), low_span)
            att_ref[0, qb * QB : (qb + 1) * QB, cols] = att.astype(BF)
            lse = top + jnp.log(total)
            totals = jnp.where(lane == 2 * pair, lse[:QB], totals)
            totals = jnp.where(lane == 2 * pair + 1, lse[QB:], totals)
        lse_ref[0, qb * QB : (qb + 1) * QB] = totals


def attend(info, x, left, right, gain, tables, parts):
    seqs, block, width = x.shape
    span = block + 2 * HALF
    pairs = width // LANES

    def seq(shape):
        return pl.BlockSpec((1,) + shape, lambda s, _: (s,) + (0,) * len(shape))

    def whole(shape):
        return pl.BlockSpec(shape, lambda s, _: (0,) * len(shape))

    table = whole((span, LANES))
    out = lambda *shape, t=BF: jax.ShapeDtypeStruct((seqs,) + shape, t)
    score_shape = (pairs, block // QB, 2 * QB, QB + 2 * HALF)
    return pl.pallas_call(
        attend_kernel,
        grid_spec=pltpu.PrefetchScalarGridSpec(
            num_scalar_prefetch=1,
            grid=(seqs,),
            in_specs=[
                seq((block, width)),
                seq((HALF, width)),
                seq((HALF, width)),
                whole((1, width)),
                table,
                table,
                table,
            ]
            + [ANY] * 4,
            out_specs=[
                seq((span, width)),
                seq((span, width)),
                seq((span, width)),
                seq((block, width)),
                seq(score_shape),
                seq((block, LANES)),
                seq((block, width)),
                whole((3 * width, width)),
            ],
            scratch_shapes=[
                pltpu.VMEM((span, width), BF),
                pltpu.SemaphoreType.DMA((4,)),
            ],
        ),
        out_shape=[
            out(span, width),
            out(span, width),
            out(span, width),
            out(block, width),
            out(*score_shape),
            out(block, LANES, t=F32),
            out(block, width),
            jax.ShapeDtypeStruct((3 * width, width), BF),
        ],
        compiler_params=params(),
        cost_estimate=cost(seqs * span * width * width * 8, 30e6, 4e6),
        name="attend",
    )(info, x, left, right, gain, *tables, *parts)


def feed_kernel(
    hidden, info, x_ref, att_ref, cot_ref, lse_ref, gain_ref, ind_ref, *rest
):
    (
        output_ref,
        normed_ref,
        mixed_ref,
        inner_ref,
        grad_ref,
        branch_ref,
        dom_ref,
        gain_grad_ref,
        full,
        sems,
    ) = rest[4:]
    width = x_ref.shape[2]
    in_w = full.at[pl.ds(0, 2 * hidden)]
    down_w = full.at[pl.ds(2 * hidden, hidden)]
    out_w = full.at[pl.ds(3 * hidden, width)]
    first_step = pl.program_id(0) == 0

    @pl.when(first_step)
    def _():
        load(info[0], rest[:4], full, sems, (hidden // 2, hidden // 4, width // 4))
        gain_grad_ref[...] = jnp.zeros_like(gain_grad_ref)

    attended = att_ref[0]
    hidden1 = x_ref[0].astype(F32) + nn(attended, out_w[...])
    normal, inverse = stats_of(hidden1)
    normed = (normal * gain_ref[...]).astype(BF)
    normed_ref[0] = normed
    cot = cot_ref[0]
    result = hidden1
    normed_grad = jnp.zeros_like(hidden1)
    step = 384
    for c in range(hidden // step):
        one = slice(c * step, (c + 1) * step)
        two = slice(hidden + c * step, hidden + (c + 1) * step)
        first = nt(normed, in_w[one])
        second = nt(normed, in_w[two])
        phi = 0.5 * (1.0 + lax.erf(first * (1.0 / math.sqrt(2.0))))
        active = first * phi
        slope = phi + first * jnp.exp(-0.5 * first * first) * (1.0 / math.sqrt(2.0 * math.pi))
        mixed = (active * second).astype(BF)
        mixed_ref[0, :, one] = mixed
        result = result + nn(mixed, down_w[one])
        mixed_grad = nt(cot, down_w[one])
        grad_one = (mixed_grad * second * slope).astype(BF)
        grad_two = (mixed_grad * active).astype(BF)
        inner_ref[0, :, one] = grad_one
        inner_ref[0, :, two] = grad_two
        normed_grad = normed_grad + nn(grad_one, in_w[one]) + nn(grad_two, in_w[two])
    output_ref[0] = result.astype(BF)
    gain_grad_ref[...] += jnp.sum(normed_grad * normal, 0, keepdims=True)
    scaled = normed_grad * gain_ref[...]
    hidden1_grad = cot.astype(F32) + inverse * (
        scaled
        - jnp.mean(scaled, -1, keepdims=True)
        - normal * jnp.mean(scaled * normal, -1, keepdims=True)
    )
    grad_ref[0] = hidden1_grad
    branch = hidden1_grad.astype(BF)
    branch_ref[0] = branch
    att_grad = nt(branch, out_w[...]).astype(BF)
    dom_ref[0, :, :width] = att_grad
    product = att_grad.astype(F32) * attended.astype(F32)
    high = product.astype(BF)
    rest_of = (product - high.astype(F32)).astype(BF)
    delta = nn(high, ind_ref[...]) + nn(rest_of, ind_ref[...])
    both = delta + lse_ref[0]
    high = both.astype(BF)
    rest_of = both - high.astype(F32)
    dom_ref[0, :, width:] = (high.astype(F32) + pltpu.roll(rest_of, 32, 1)).astype(BF)


def feed(info, x, att, cot, lse, gain, ind, parts):
    seqs, block, width = x.shape
    hidden = parts[0].shape[0] - width // 4
    hidden = 4 * hidden // 3

    def seq(*shape):
        return pl.BlockSpec((1,) + shape, lambda s, _: (s,) + (0,) * len(shape))

    def whole(*shape):
        return pl.BlockSpec(shape, lambda s, _: (0,) * len(shape))

    out = lambda *shape, t=BF: jax.ShapeDtypeStruct((seqs,) + shape, t)
    return pl.pallas_call(
        functools.partial(feed_kernel, hidden),
        grid_spec=pltpu.PrefetchScalarGridSpec(
            num_scalar_prefetch=1,
            grid=(seqs,),
            in_specs=[
                seq(block, width),
                seq(block, width),
                seq(block, width),
                seq(block, LANES),
                whole(1, width),
                whole(width, LANES),
            ]
            + [ANY] * 4,
            out_specs=[
                seq(block, width),
                seq(block, width),
                seq(block, hidden),
                seq(block, 2 * hidden),
                seq(block, width),
                seq(block, width),
                seq(block, width + LANES),
                whole(1, width),
            ],
            scratch_shapes=[
                pltpu.VMEM((3 * hidden + width, width), BF),
                pltpu.SemaphoreType.DMA((12,)),
            ],
        ),
        out_shape=[
            out(block, width),
            out(block, width),
            out(block, hidden),
            out(block, 2 * hidden),
            out(block, width, t=F32),
            out(block, width),
            out(block, width + LANES),
            jax.ShapeDtypeStruct((1, width), F32),
        ],
        compiler_params=params(),
        cost_estimate=cost(seqs * block * width * (4 * width + 12 * hidden), 30e6, 3e6),
        name="feed",
    )(info, x, att, cot, lse, gain, ind, *parts)


def attend_back_kernel(
    q_ref,
    k_ref,
    v_ref,
    p_ref,
    dom_ref,
    left_ref,
    right_ref,
    cos_ref,
    sa_ref,
    sb_ref,
    *rest,
):
    grad_ref = rest[-1]
    block = dom_ref.shape[1]
    width = q_ref.shape[2]
    span = block + 2 * HALF
    pairs = width // LANES
    scale = HEAD**-0.5
    low = lax.broadcasted_iota(jnp.int32, (QB, LANES), 1) < HEAD
    row = lax.broadcasted_iota(jnp.int32, (QB, QB), 0)
    col = lax.broadcasted_iota(jnp.int32, (QB, QB), 1)
    seen = ((row < HALF) & (col <= row)) | ((row >= HALF) & (col >= row))
    seen = jnp.concatenate([seen, seen], 0)
    stats = jnp.concatenate([left_ref[0, :, width:], right_ref[0, :, width:]], 0).astype(F32)
    stats = stats + pltpu.roll(stats, LANES - 32, 1)
    far = slice(HALF + block, span)
    near_left = slice(HALF, 2 * HALF)
    near_right = slice(block, block + HALF)
    blocks = block // QB
    for pair in range(pairs):
        cols = slice(pair * LANES, (pair + 1) * LANES)
        key_parts, value_parts = [], []
        for qb in range(blocks):
            own = slice(HALF + qb * QB, HALF + (qb + 1) * QB)
            keys = slice(qb * QB, (qb + 1) * QB + 2 * HALF)
            rows = slice(qb * QB, (qb + 1) * QB)
            soft = p_ref[0, pair, qb]
            att_grad = two_heads(dom_ref[0, rows, cols], low)
            soft_grad = nt(att_grad, v_ref[0, keys, cols])
            soft_wide = soft.astype(F32)
            delta = jnp.sum(soft_wide * soft_grad, -1, keepdims=True)
            score_grad = (soft_wide * (soft_grad - delta)).astype(BF)
            query_grad = one_pair(nn(score_grad, k_ref[0, keys, cols]), low) * scale
            grad_ref[0, rows, cols] = turn(
                query_grad, cos_ref[rows], sa_ref[rows], sb_ref[rows], True
            ).astype(BF)
            key_parts.append(tn(score_grad, two_heads(q_ref[0, own, cols], low)))
            value_parts.append(tn(soft, att_grad))
        far_q = two_heads(jnp.concatenate([q_ref[0, :HALF, cols], q_ref[0, far, cols]], 0), low)
        far_grad = two_heads(
            jnp.concatenate([left_ref[0, :, cols], right_ref[0, :, cols]], 0), low
        )
        near_k = jnp.concatenate([k_ref[0, near_left, cols], k_ref[0, near_right, cols]], 0)
        near_v = jnp.concatenate([v_ref[0, near_left, cols], v_ref[0, near_right, cols]], 0)
        h = 2 * pair
        lse = jnp.concatenate([stats[:, h : h + 1], stats[:, h + 1 : h + 2]], 0)
        delta = jnp.concatenate([stats[:, 64 + h : 65 + h], stats[:, 65 + h : 66 + h]], 0)
        soft = jnp.where(seen, jnp.exp(jnp.where(seen, nt(far_q, near_k) - lse, 0.0)), 0.0)
        score_grad = (soft * (nt(far_grad, near_v) - delta)).astype(BF)
        far_key = tn(score_grad, far_q)
        far_value = tn(soft.astype(BF), far_grad)
        for base, pieces, extra in ((width, key_parts, far_key), (2 * width, value_parts, far_value)):
            total = jnp.zeros((span, LANES), F32)
            for qb in range(blocks):
                before, after = qb * QB, span - (qb + 1) * QB - 2 * HALF
                piece = pieces[qb]
                if before:
                    piece = jnp.concatenate([jnp.zeros((before, LANES), F32), piece], 0)
                if after:
                    piece = jnp.concatenate([piece, jnp.zeros((after, LANES), F32)], 0)
                total = total + piece
            own = total[HALF : HALF + block]
            own = jnp.concatenate(
                [
                    own[:HALF] + extra[:HALF],
                    own[HALF : block - HALF],
                    own[block - HALF :] + extra[HALF:],
                ],
                0,
            )
            if base == width:
                own = turn(own, cos_ref[...], sa_ref[...], sb_ref[...], True)
            grad_ref[0, :, base + pair * LANES : base + (pair + 1) * LANES] = own.astype(BF)


def attend_back(q, k, v, p, dom, left, right, tables, start, count, before):
    seqs, block, _ = dom.shape
    span, width = q.shape[1:]

    def seq(*shape):
        return pl.BlockSpec((1,) + shape, lambda s: (s + start,) + (0,) * len(shape))

    table = pl.BlockSpec((block, LANES), lambda s: (0, 0))
    return pl.pallas_call(
        attend_back_kernel,
        grid=(count,),
        in_specs=[
            seq(span, width),
            seq(span, width),
            seq(span, width),
            seq(*p.shape[1:]),
            seq(block, width + LANES),
            seq(HALF, width + LANES),
            seq(HALF, width + LANES),
            table,
            table,
            table,
        ]
        + [ANY] * len(before),
        out_specs=seq(block, 3 * width),
        out_shape=jax.ShapeDtypeStruct((seqs, block, 3 * width), BF),
        input_output_aliases={10: 0} if before else {},
        compiler_params=params(),
        cost_estimate=cost(count * block * span * width * 12, 7e6 * count, 3e5 * count),
        name="attend_back",
    )(q, k, v, p, dom, left, right, *tables, *before)


EXTRA = 32


def weight_grad_kernel(steps, n, with_gains, info, *refs):
    pairs = len(steps)
    operands = refs[: 2 * pairs]
    keep, send, full, sems = refs[-6:-2] if with_gains else refs[-4:]
    i = pl.program_id(0)
    last = i == pl.num_programs(0) - 1
    stride = keep.shape[0] // (n // 2)
    copies, done, taken = [], 0, 0

    def target(j, row, rows):
        return (send if j % 2 else keep).at[pl.ds((j // 2) * stride + row, rows)]

    for a, count in enumerate(steps):
        lhs, rhs = operands[2 * a : 2 * a + 2]
        step = lhs.shape[1]

        @pl.when((i >= done) & (i < done + count))
        def _():
            total = tn(lhs[...], rhs[...])
            full[pl.ds(pl.multiple_of(i * step, step), step)] = total.astype(BF)
            if with_gains:
                weight = refs[2 * pairs]
                gain_total = refs[-2]
                part = jnp.sum(total * weight[...].astype(F32), 0, keepdims=True)
                gain_total[...] = jnp.where(i == 0, part, gain_total[...] + part)

        rows = count * step // n
        for j in range(n):
            source = pl.multiple_of(done * step + (info[0] ^ j) * rows, 16)
            copies.append(
                pltpu.make_async_copy(
                    full.at[pl.ds(source, rows)], target(j, taken, rows), sems.at[len(copies)]
                )
            )
        done += count
        taken += rows
    if with_gains:
        for j in range(n):
            copies.append(
                pltpu.make_async_copy(refs[-1], target(j, taken, EXTRA), sems.at[len(copies)])
            )

    @pl.when(last)
    def _():
        if with_gains:
            gain, feed_grad = refs[2 * pairs + 1 : 2 * pairs + 3]
            gain_total, gain_rows = refs[-2:]
            row = lax.broadcasted_iota(jnp.int32, gain_rows.shape, 0)
            value = jnp.where(row == 0, gain_total[...] / gain[...], 0.0)
            gain_rows[...] = jnp.where(row == 1, feed_grad[...], value).astype(BF)
        start_all(copies)


def weight_grad(info, pairs, n, gains=()):
    tokens, width = pairs[0][1].shape
    step = 384
    steps = tuple(lhs.shape[1] // step for lhs, _ in pairs)
    total = sum(steps)
    specs, done = [], 0
    for count in steps:
        low, high = done, done + count - 1
        specs.append(
            pl.BlockSpec(
                (tokens, step),
                lambda i, _, low=low, high=high: (0, jnp.clip(i, low, high) - low),
            )
        )
        specs.append(pl.BlockSpec((tokens, width), lambda i, _: (0, 0)))
        done += count
    m = total * step
    scratch = [
        pltpu.VMEM((m, width), BF),
        pltpu.SemaphoreType.DMA((n * (len(pairs) + bool(gains)),)),
    ]
    if gains:
        specs.append(pl.BlockSpec((step, width), lambda i, _: (i, 0)))
        specs += [pl.BlockSpec((1, width), lambda i, _: (0, 0))] * 2
        scratch += [pltpu.VMEM((1, width), F32), pltpu.VMEM((EXTRA, width), BF)]
    rows = m // n + (EXTRA if gains else 0)
    return pl.pallas_call(
        functools.partial(weight_grad_kernel, steps, n, bool(gains)),
        grid_spec=pltpu.PrefetchScalarGridSpec(
            num_scalar_prefetch=1,
            grid=(total,),
            in_specs=specs,
            out_specs=[ANY] * 2,
            scratch_shapes=scratch,
        ),
        out_shape=[jax.ShapeDtypeStruct((n // 2 * rows, width), BF)] * 2,
        compiler_params=params(),
        cost_estimate=cost(2 * tokens * m * width, 2 * (tokens * (m + width) + m * width)),
        name="weight_grad",
    )(info, *[a for pair in pairs for a in pair], *gains)


def input_kernel(grad_ref, x_ref, gain_ref, hidden_ref, weight_ref, *rest):
    out_ref = rest[-1]
    normed_grad = nn(grad_ref[0], weight_ref[...])
    normal, inverse = stats_of(x_ref[0].astype(F32))
    scaled = normed_grad * gain_ref[...]
    out_ref[0] = hidden_ref[0] + inverse * (
        scaled
        - jnp.mean(scaled, -1, keepdims=True)
        - normal * jnp.mean(scaled * normal, -1, keepdims=True)
    )


def input_back(grad, x, gain, hidden_grad, weight, start, count, before):
    seqs, block, width = x.shape

    def seq(*shape):
        return pl.BlockSpec((1,) + shape, lambda s: (s + start,) + (0,) * len(shape))

    def whole(*shape):
        return pl.BlockSpec(shape, lambda s: (0,) * len(shape))

    return pl.pallas_call(
        input_kernel,
        grid=(count,),
        in_specs=[
            seq(block, 3 * width),
            seq(block, width),
            whole(1, width),
            seq(block, width),
            whole(3 * width, width),
        ]
        + [ANY] * len(before),
        out_specs=seq(block, width),
        out_shape=jax.ShapeDtypeStruct((seqs, block, width), F32),
        input_output_aliases={5: 0} if before else {},
        compiler_params=params(),
        cost_estimate=cost(count * block * width * width * 6, 4e6 * count),
        name="input_back",
    )(grad, x, gain, hidden_grad, weight, *before)


def swap(value, axis, bit):
    count = lax.axis_size(axis)
    return lax.ppermute(value, axis, [(i, i ^ bit) for i in range(count)])


def bits_of(axis):
    count = lax.axis_size(axis)
    return [1 << b for b in range(count.bit_length() - 1)]


def tie(*values):
    return lax.optimization_barrier(values)


def plus(a, b):
    return (a.astype(F32) + b.astype(F32)).astype(BF)


def swap_both(value, context_bit, bit):
    count = lax.axis_size("wa")
    every = lax.axis_size("ctx") * count
    mask = context_bit * count + bit
    return lax.ppermute(value, ("ctx", "wa"), [(i, i ^ mask) for i in range(every)])


def reduce_steps(keep, send, far_first):
    place = lax.axis_index("ctx") & 3
    got = yield [swap(send, "wa", 1)]
    both = plus(keep, got[0])
    size = both.shape[0] // 2
    own, far = both[:size], both[size:]
    groups = [(own, 0), (far, 2)]
    if far_first:
        got = yield [swap(far, "wa", 2)]
        own = plus(own, got[0])
        groups = [(own, 0)]
    quarter = size // 4
    cut = lambda a, t: lax.dynamic_slice_in_dim(a, (place ^ t) * quarter, quarter, 0)
    got = yield [
        swap_both(cut(a, t), t, bit) for a, bit in groups for t in range(4) if bit or t
    ]
    terms = [a.astype(F32) for a in [cut(own, 0)] + list(got)]
    value = terms[0] + terms[1] + terms[2] + terms[3]
    if not far_first:
        value = value + (terms[4] + terms[5] + terms[6] + terms[7])
    value = value.astype(BF)
    for bit in bits_of("ctx")[2:]:
        got = yield [swap(value, "ctx", bit)]
        value = plus(value, got[0])
    got = yield [swap(value, "ctx", t) for t in range(1, 4)]
    quarters = jnp.stack([value] + list(got))
    rows = [lax.dynamic_index_in_dim(quarters, place ^ t, 0, keepdims=False) for t in range(4)]
    return jnp.concatenate(rows, 0).astype(F32)


class Chains:
    def __init__(self):
        self.running, self.flying, self.results = {}, {}, {}

    def start(self, name, steps):
        self.running[name] = steps
        self.flying[name] = next(steps)

    def step(self, names, *values):
        names = [name for name in names if name in self.running]
        flying, values = tie([self.flying[name] for name in names], values)
        for name, got in zip(names, flying, strict=True):
            try:
                self.flying[name] = self.running[name].send(got)
            except StopIteration as end:
                self.results[name] = end.value
                del self.running[name]
        return values


def neighbours(value):
    count = lax.axis_size("ctx")
    ends = count - 1
    left = lax.ppermute(value[:, -HALF:], "ctx", [(i, i + 1) for i in range(ends)])
    right = lax.ppermute(value[:, :HALF], "ctx", [(i + 1, i) for i in range(ends)])
    return left, right


def local(
    layer_input, cotangent, attention_gain, qkv_proj, out_proj, feed_gain, in_proj, down_proj
):
    seqs, block, width = layer_input.shape
    rows = seqs * block
    heads = width // HEAD
    n = lax.axis_size("wa")
    context_rank = lax.axis_index("ctx")
    seq_len = block * lax.axis_size("ctx")
    place = context_rank & 3
    info = jnp.stack(
        [
            lax.axis_index("wa").astype(jnp.int32),
            context_rank.astype(jnp.int32),
            jnp.int32(seq_len),
            place.astype(jnp.int32),
        ]
    )
    frequencies = jnp.power(10000.0, -jnp.arange(0, HEAD, 2, dtype=F32) / HEAD)
    places = context_rank * block - HALF + jnp.arange(block + 2 * HALF, dtype=jnp.int32)
    angles = places.astype(F32)[:, None] * frequencies[None, :]
    cosine, sine = jnp.cos(angles), jnp.sin(angles)
    zero = jnp.zeros_like(sine)
    tables = (
        jnp.concatenate([cosine] * 4, -1),
        jnp.concatenate([-sine, zero] * 2, -1),
        jnp.concatenate([zero, sine] * 2, -1),
    )
    own_tables = tuple(t[HALF : HALF + block] for t in tables)
    lane = jnp.arange(LANES, dtype=jnp.int32)[None, :]
    head_of = jnp.arange(width, dtype=jnp.int32)[:, None] // HEAD
    ind = (lane == head_of + 64).astype(BF)

    quarter = down_proj.shape[0]
    far = lambda value: swap(value, "wa", 2)
    near = lambda value: swap(value, "wa", 1)
    left, right = neighbours(layer_input)
    qkv_own = qkv_proj.T
    qkv_far, qkv_near = far(qkv_own), near(qkv_own)
    rest_own = jnp.concatenate([in_proj.T, down_proj, out_proj], 0)
    qkv_far, qkv_near, left, right, rest_own, tables, own_tables, ind, info = tie(
        qkv_far, qkv_near, left, right, rest_own, tables, own_tables, ind, info
    )
    qkv_both = near(qkv_far)
    rest_far, rest_near = far(rest_own), near(rest_own)
    qkv_parts = [qkv_own, qkv_near, qkv_far, qkv_both]

    gain1 = attention_gain[None]
    made = attend(info, layer_input, left, right, gain1, tables, qkv_parts)
    made, rest_near, rest_far = tie(made, rest_near, rest_far)
    q, k, v, attended, soft, lse, normed1, qkv_weight = made
    rest_parts = [rest_own, rest_near, rest_far, near(rest_far)]
    output, normed2, mixed, inner_grad, hidden_grad, branch, dom, feed_gain_grad = feed(
        info, layer_input, attended, cotangent, lse, feed_gain[None], ind, rest_parts
    )
    left_grad, right_grad = neighbours(dom)
    flat = lambda a: a.reshape(rows, a.shape[-1])
    chains = Chains()
    in_parts = weight_grad(info, [(flat(inner_grad), flat(normed2))], n)
    in_parts, mixed, branch, left_grad = tie(in_parts, mixed, branch, left_grad)
    chains.start("in", reduce_steps(*in_parts, True))
    other_parts = weight_grad(
        info, [(flat(mixed), flat(cotangent)), (flat(attended), flat(branch))], n
    )
    other_parts, q, right_grad = chains.step(["in"], other_parts, q, right_grad)
    chains.start("other", reduce_steps(*other_parts, True))
    (q,) = chains.step(["other"], q)
    half_seqs = seqs // 2
    back = attend_back(
        q, k, v, soft, dom, left_grad, right_grad, own_tables, 0, half_seqs, ()
    )
    back, q = chains.step(["in"], back, q)
    back = attend_back(
        q, k, v, soft, dom, left_grad, right_grad, own_tables, half_seqs, seqs - half_seqs, (back,)
    )
    (back,) = chains.step(["in", "other"], back)
    qkv_back = weight_grad(
        info, [(flat(back), flat(normed1))], n, (qkv_weight, gain1, feed_gain_grad)
    )
    qkv_back, back = chains.step(["in", "other"], qkv_back, back)
    chains.start("qkv", reduce_steps(*qkv_back, False))
    made = input_back(back, layer_input, gain1, hidden_grad, qkv_weight, 0, half_seqs, ())
    made, back = chains.step(["in", "other", "qkv"], made, back)
    input_grad = input_back(
        back, layer_input, gain1, hidden_grad, qkv_weight, half_seqs, seqs - half_seqs, (made,)
    )
    (input_grad,) = chains.step(["in", "other"], input_grad)
    while chains.running:
        chains.step(list(chains.running))
    qkv_grad, in_grad, other_grad = (chains.results[name] for name in ("qkv", "in", "other"))
    qkv_rows = qkv_proj.shape[1]
    gains = qkv_grad[qkv_rows : qkv_rows + 2]
    qkv_grad = qkv_grad[:qkv_rows]
    down_grad, out_grad = other_grad[:quarter], other_grad[quarter:]
    return (
        output,
        input_grad,
        gains[0],
        gains[1],
        qkv_grad.T,
        out_grad,
        in_grad.T,
        down_grad,
    )


def solution(mesh):
    return jax.shard_map(
        local,
        mesh=mesh,
        in_specs=(
            P("wa", "ctx", None),
            P("wa", "ctx", None),
            P(),
            P(None, "wa"),
            P("wa", None),
            P(),
            P(None, "wa"),
            P("wa", None),
        ),
        out_specs=(
            P("wa", "ctx", None),
            P("wa", "ctx", None),
            P(),
            P(),
            P(None, "wa"),
            P("wa", None),
            P(None, "wa"),
            P("wa", None),
        ),
        check_vma=False,
    )
```
